512 devices in a mesh: cand: 64 (over x, z, core), feat: 8 (over y).
Axes of the slice: x: 4, y: 8, z: 8, core: 2. Of those that a mesh axis runs over, the one named last changes fastest.
Arguments:
- behaviour: float32 [65536, 4096], P('cand', 'feat'), may hold values from 0.2 to 4500, as said below
- panel: float32 [4096, 64], P('feat'), may hold values from -6 to 6
Outputs:
- left_vectors: float32 [65536, 64], P('cand')
- right_vectors: float32 [4096, 64], P('feat')
The draws below stay inside these ranges and needn't reach their ends.
Inputs may be any that keep to these rules, and one draw needn't show every extreme that they name: `behaviour`: every entry is positive.
All inputs are finite; a program needn't handle non-finite values.
Results may differ from the reference program's by a relative error of at most 0.00017.
Values sent between devices are 32-bit elements; how exact they have to be, the bound alone decides.
No kernel may reach another device: no remote copies, remote signals or barrier semaphores. Data moves between devices by JAX's collectives and lax.ppermute only.
A program may use at most 64 MiB of HBM per device.

```python
import math
import jax
import jax.numpy as jnp
from jax import lax

FEATURES = 4096
RANK = 64
CANDIDATES = 65536


def draw_behaviour(key, part):
    key_rows, key_cols, key_noise = jax.random.split(key, 3)
    row_pos = jnp.arange(CANDIDATES, dtype=jnp.float32)[:, None] / CANDIDATES
    col_pos = jnp.arange(FEATURES, dtype=jnp.float32)[None, :] / FEATURES
    row_factor = jnp.exp(jax.random.uniform(key_rows, (CANDIDATES, 1), jnp.float32, 0.0, math.log(10.0))) * (1.0 + 2.0 * row_pos)
    col_factor = jnp.exp(jax.random.uniform(key_cols, (1, FEATURES), jnp.float32, 0.0, math.log(10.0))) * (1.0 + 2.0 * col_pos)
    noise = jnp.exp(jax.random.uniform(key_noise, (CANDIDATES, FEATURES), jnp.float32, math.log(0.2), math.log(5.0)))
    return (row_factor * col_factor * noise).astype(jnp.float32)


def block_scale(rng, extent, pieces, smallest, high):
    loudness, own = 1.0, jax.random.fold_in(rng, 6)
    for axis_at, parts in pieces:
        steps = jnp.exp(jax.random.uniform(jax.random.fold_in(own, axis_at), (parts,), jnp.float32, smallest / len(pieces), high / len(pieces)))
        loudness = loudness * jnp.repeat(steps, extent[axis_at] // parts).reshape([-1 if axis == axis_at else 1 for axis in range(len(extent))])
    return loudness


def centred(stream_key, dims, spread, reach, pieces=(), held_as=jnp.bfloat16):
    drawn = spread * jax.random.normal(stream_key, dims, jnp.float32)
    if pieces:
        drawn = drawn * block_scale(stream_key, dims, pieces, -0.22, 0.18)
    return jnp.clip(drawn, -reach, reach).astype(held_as)


def setup_inputs(seed: int = 0) -> dict:
    key_list = jax.random.split(jax.random.key(seed), 3)
    return {
        "behaviour": draw_behaviour(jax.random.fold_in(key_list[2], 71), 0),
        "panel": centred(key_list[1], (FEATURES, RANK), 1.0, 6.0, ((0, 8),), jnp.float32),
    }


def reference(behaviour, panel):
    highest = lax.Precision.HIGHEST
    row_deg = lax.optimization_barrier(jnp.sum(behaviour, axis=1))
    col_deg = lax.optimization_barrier(jnp.sum(behaviour, axis=0))
    row_scale = lax.rsqrt(row_deg)
    col_scale = lax.rsqrt(col_deg)
    raw_panel = jnp.dot(behaviour.astype(jnp.float32), (panel * col_scale[:, None]).astype(jnp.float32), precision=highest, preferred_element_type=jnp.float32) * row_scale[:, None]
    gram = jnp.dot(raw_panel.T.astype(jnp.float32), raw_panel.astype(jnp.float32), precision=highest, preferred_element_type=jnp.float32)
    factor = jnp.linalg.cholesky(gram)
    left_vectors = lax.linalg.triangular_solve(factor, raw_panel, left_side=False, lower=True, transpose_a=True)
    weighted = left_vectors * row_scale[:, None]
    right_vectors = lax.dot_general(behaviour.astype(jnp.float32), weighted.astype(jnp.float32), (((0,), (0,)), ((), ())), precision=highest, preferred_element_type=jnp.float32) * col_scale[:, None]
    return (left_vectors, right_vectors)
```

```python
import jax
import jax.numpy as jnp
from jax import lax
from jax.sharding import PartitionSpec as P

RANK = 64


def dot(a, b, dims):
    return lax.dot_general(
        a, b, (dims, ((), ())), precision=lax.Precision.HIGHEST, preferred_element_type=jnp.float32
    )


def exchange(x, axis):
    return lax.all_to_all(x, axis, 0, 0)


def spread(x, axis, n):
    return exchange(jnp.broadcast_to(x[None], (n,) + x.shape), axis)


def body(behaviour, panel):
    cands, feats = lax.axis_size("cand"), lax.axis_size("feat")
    rows, cols = behaviour.shape
    row_part = jnp.sum(behaviour, axis=1)
    col_part = jnp.sum(behaviour, axis=0)
    col_deg = jnp.sum(spread(col_part.reshape(-1, 128), "cand", cands), axis=0).reshape(cols)
    col_scale = lax.rsqrt(col_deg)

    part = dot(panel.T * col_scale[None, :], behaviour, ((1,), (1,)))
    part = jnp.concatenate([part, row_part[None, :], jnp.zeros((7, rows), jnp.float32)], axis=0)
    part = part.reshape(RANK + 8, feats, rows // feats).transpose(1, 0, 2)
    mine = jnp.sum(exchange(part, "feat"), axis=0)
    scale = lax.rsqrt(mine[RANK : RANK + 1])
    mine = jnp.concatenate([mine[:RANK] * scale, jnp.broadcast_to(scale, (8,) + scale.shape[1:])], axis=0)
    whole = spread(mine, "feat", feats).transpose(1, 0, 2).reshape(RANK + 8, rows)
    raw, row_scale = whole[:RANK], whole[RANK : RANK + 1]

    gram = dot(raw, raw, ((1,), (1,)))
    right = dot(raw * row_scale, behaviour, ((1,), (0,)))
    gram = jnp.pad(gram, ((0, 0), (0, 128 - RANK)))
    both = jnp.concatenate([right.reshape(RANK, -1, 128), gram[:, None, :]], axis=1)
    line = jnp.sum(exchange(both, "cand"), axis=0)
    both = spread(line, "cand", cands)
    gram = both[:, -1, :RANK]
    right = both[:, :-1, :].reshape(RANK, cols) * col_scale[None, :]
    factor = jnp.linalg.cholesky(gram)
    inverse = lax.linalg.triangular_solve(
        factor, jnp.eye(RANK, dtype=jnp.float32), left_side=True, lower=True
    )
    left = dot(inverse, raw, ((1,), (0,)))
    right = dot(inverse, right, ((1,), (0,)))
    return (left.T, right.T)


def solution(mesh):
    in_specs = (P("cand", "feat"), P("feat", None))
    out_specs = (P("cand", None), P("feat", None))
    return jax.shard_map(body, mesh=mesh, in_specs=in_specs, out_specs=out_specs, check_vma=False)
```

```python
import jax
import jax.numpy as jnp
from jax import lax
from jax.experimental import pallas as pl
from jax.experimental.pallas import tpu as pltpu
from jax.sharding import Mesh, PartitionSpec as P

RANK = 64
PAD = RANK + 8
LANES = 128
GRID = (4, 8, 2)
NT = (((1,), (1,)), ((), ()))
NN = (((1,), (0,)), ((), ()))


def split(a):
    high = a.astype(jnp.bfloat16)
    low = (a - high.astype(jnp.float32)).astype(jnp.bfloat16)
    return high, low


def product(a, b, dims):
    m = a[0].shape[0]
    stacked = jnp.concatenate([a[0], a[1]], axis=0)
    full = lax.dot_general(stacked, b[0], dims, preferred_element_type=jnp.float32)
    rest = lax.dot_general(a[0], b[1], dims, preferred_element_type=jnp.float32)
    return full[:m] + (full[m:] + rest)


def call(kernel, out_shape, operands, name, flops, nbytes):
    return pl.pallas_call(
        kernel,
        out_shape=out_shape,
        name=name,
        in_specs=[pl.BlockSpec(memory_space=pltpu.VMEM)] * len(operands),
        out_specs=jax.tree.map(lambda _: pl.BlockSpec(memory_space=pltpu.VMEM), out_shape),
        cost_estimate=pl.CostEstimate(flops=flops, bytes_accessed=nbytes, transcendentals=0),
        compiler_params=pltpu.CompilerParams(vmem_limit_bytes=24 << 20),
    )(*operands)


def column_kernel(b_ref, out_ref):
    copies, parts, _ = out_ref.shape
    sums = jnp.sum(b_ref[...], axis=0, keepdims=True)
    rows = jnp.concatenate([sums[:, LANES * i : LANES * (i + 1)] for i in range(parts)], axis=0)
    out_ref[...] = jnp.broadcast_to(rows[None], out_ref.shape)


def project_kernel(b_ref, panel_ref, sums_ref, out_ref, scale_ref):
    parts = sums_ref.shape[1]
    deg = jnp.sum(sums_ref[...], axis=0)
    deg = jnp.concatenate([deg[i : i + 1] for i in range(parts)], axis=1)
    scale = lax.rsqrt(deg)
    scale_ref[...] = scale
    ones = jnp.ones((PAD - RANK, deg.shape[1]), jnp.float32)
    left = split(jnp.concatenate([panel_ref[...] * scale, ones], axis=0))
    for i in range(out_ref.shape[0]):
        out_ref[i] = product(left, split(b_ref[LANES * i : LANES * (i + 1), :]), NT)


def normalise_kernel(parts_ref, out_ref):
    total = jnp.sum(parts_ref[...], axis=0)
    scale = lax.rsqrt(total[RANK:])
    out = jnp.concatenate([total[:RANK] * scale[:1], scale], axis=0)
    out_ref[...] = jnp.broadcast_to(out[None], out_ref.shape)


def reduce_kernel(b_ref, whole_ref, out_ref):
    chunks = whole_ref.shape[0]
    raw = jnp.concatenate([whole_ref[i, :RANK, :] for i in range(chunks)], axis=1)
    scale = jnp.concatenate([whole_ref[i, RANK : RANK + 1, :] for i in range(chunks)], axis=1)
    cols = b_ref.shape[1]
    out_ref[:, :cols] = product(split(raw * scale), split(b_ref[...]), NN)
    gram = lax.dot_general(
        raw, raw, NT, precision=lax.Precision.HIGHEST, preferred_element_type=jnp.float32
    )
    out_ref[:, cols:] = jnp.concatenate([gram, jnp.zeros((RANK, LANES - RANK), jnp.float32)], axis=1)


def finish_kernel(both_ref, whole_ref, scale_ref, left_ref, right_ref):
    chunks = whole_ref.shape[0]
    cols = scale_ref.shape[1]
    sub = lax.broadcasted_iota(jnp.int32, (8, LANES), 0)
    lane = lax.broadcasted_iota(jnp.int32, (8, LANES), 1)
    work = [
        jnp.where(
            lane < RANK, both_ref[8 * b : 8 * b + 8, cols:], (lane == RANK + 8 * b + sub).astype(jnp.float32)
        )
        for b in range(RANK // 8)
    ]
    roots = [None] * (RANK // 8)
    for k in range(RANK):
        at, s = divmod(k, 8)
        row = work[at][s : s + 1, :]
        pivot = row[:, k : k + 1]
        scaled = row * (1.0 / pivot)
        root = jnp.broadcast_to(lax.rsqrt(pivot), (8, LANES))
        roots[at] = root if s == 0 else jnp.where(sub == s, root, roots[at])
        for b in range(at, RANK // 8):
            column = work[b][:, k : k + 1]
            if b == at:
                column = jnp.where(sub[:, :1] > s, column, 0.0)
            work[b] = work[b] - column * scaled
    inverse = jnp.concatenate([work[b] * roots[b] for b in range(RANK // 8)], axis=0)[:, RANK:]
    inverse = split(inverse)
    for i in range(chunks):
        left_ref[:, LANES * i : LANES * (i + 1)] = product(inverse, split(whole_ref[i, :RANK, :]), NN)
    right_ref[...] = product(inverse, split(both_ref[:, :cols] * scale_ref[...]), NN)


def exchange(x, axis):
    return lax.all_to_all(x, axis, 0, 0)


def spread(x, axis, n):
    return exchange(jnp.broadcast_to(x[None], (n,) + x.shape), axis)


def body(behaviour, panel):
    x, z, core = GRID
    feats = lax.axis_size("feat")
    rows, cols = behaviour.shape
    cands = ("x", "z", "core")
    near = ("x", "core")
    f32 = jnp.float32
    shape = jax.ShapeDtypeStruct

    sums = call(
        column_kernel, shape((x * z * core, cols // LANES, LANES), f32), (behaviour,), "columns", rows * cols, 4 * rows * cols
    )
    sums = exchange(sums, cands)
    part, col_scale = call(
        project_kernel,
        (shape((feats, PAD, rows // feats), f32), shape((1, cols), f32)),
        (behaviour, panel.T, sums),
        "project",
        6 * rows * cols * PAD,
        4 * rows * cols,
    )
    part = exchange(part, "feat")
    mine = call(
        normalise_kernel, shape(part.shape, f32), (part,), "normalise", part.size, 8 * part.size
    )
    whole = exchange(mine, "feat")
    both = call(
        reduce_kernel, shape((RANK, cols + LANES), f32), (behaviour, whole), "reduce", 6 * rows * cols * RANK, 4 * rows * cols
    )
    both = exchange(both.reshape(x * core, -1, cols + LANES), near)
    line = jnp.sum(both, axis=0)
    line = jnp.sum(spread(line, "z", z), axis=0)
    both = spread(line, near, x * core).reshape(RANK, cols + LANES)
    left, right = call(
        finish_kernel,
        (shape((RANK, rows), f32), shape((RANK, cols), f32)),
        (both, whole, col_scale),
        "finish",
        6 * RANK * RANK * (rows + cols),
        8 * RANK * (rows + cols),
    )
    return (left.T, right.T)


def solution(mesh):
    assert GRID[0] * GRID[1] * GRID[2] == mesh.shape["cand"]
    fine = Mesh(mesh.devices.reshape(GRID + (mesh.shape["feat"],)), ("x", "z", "core", "feat"))
    cands = ("x", "z", "core")
    in_specs = (P(cands, "feat"), P("feat", None))
    out_specs = (P(cands, None), P("feat", None))
    return jax.shard_map(body, mesh=fine, in_specs=in_specs, out_specs=out_specs, check_vma=False)
```

```python
import itertools

import jax
import jax.numpy as jnp
from jax import lax
from jax.experimental import pallas as pl
from jax.experimental.pallas import tpu as pltpu
from jax.sharding import PartitionSpec as P

RANK = 64
PAD = RANK + 8
LANES = 128
GRID = (4, 8, 2)
FIRST_Y = 6
FIRST_Z = 6
NT = (((1,), (1,)), ((), ()))
NN = (((1,), (0,)), ((), ()))


def split(a):
    high = a.astype(jnp.bfloat16)
    low = (a - high.astype(jnp.float32)).astype(jnp.bfloat16)
    return high, low


def product(a, b, dims):
    m = a[0].shape[0]
    stacked = jnp.concatenate([a[0], a[1]], axis=0)
    full = lax.dot_general(stacked, b[0], dims, preferred_element_type=jnp.float32)
    rest = lax.dot_general(a[0], b[1], dims, preferred_element_type=jnp.float32)
    return full[:m] + (full[m:] + rest)


def call(kernel, out_shape, operands, name, flops, nbytes):
    return pl.pallas_call(
        kernel,
        out_shape=out_shape,
        name=name,
        in_specs=[pl.BlockSpec(memory_space=pltpu.VMEM)] * len(operands),
        out_specs=jax.tree.map(lambda _: pl.BlockSpec(memory_space=pltpu.VMEM), out_shape),
        cost_estimate=pl.CostEstimate(flops=flops, bytes_accessed=nbytes, transcendentals=0),
        compiler_params=pltpu.CompilerParams(vmem_limit_bytes=24 << 20),
    )(*operands)


def column_kernel(b_ref, out_ref):
    copies, parts, _ = out_ref.shape
    sums = jnp.sum(b_ref[...], axis=0, keepdims=True)
    rows = jnp.concatenate([sums[:, LANES * i : LANES * (i + 1)] for i in range(parts)], axis=0)
    out_ref[...] = jnp.broadcast_to(rows[None], out_ref.shape)


def project_kernel(b_ref, panel_ref, sums_ref, out_ref, scale_ref):
    parts = sums_ref.shape[1]
    deg = jnp.sum(sums_ref[...], axis=0)
    deg = jnp.concatenate([deg[i : i + 1] for i in range(parts)], axis=1)
    scale = lax.rsqrt(deg)
    scale_ref[...] = scale
    ones = jnp.ones((PAD - RANK, deg.shape[1]), jnp.float32)
    left = split(jnp.concatenate([panel_ref[...] * scale, ones], axis=0))
    for i in range(out_ref.shape[0]):
        out_ref[i] = product(left, split(b_ref[LANES * i : LANES * (i + 1), :]), NT)


def normalise_kernel(parts_ref, out_ref):
    total = jnp.sum(parts_ref[...], axis=0)
    scale = lax.rsqrt(total[RANK:])
    out = jnp.concatenate([total[:RANK] * scale[:1], scale], axis=0)
    out_ref[...] = jnp.broadcast_to(out[None], out_ref.shape)


def reduce_kernel(b_ref, whole_ref, out_ref):
    chunks = whole_ref.shape[0]
    raw = jnp.concatenate([whole_ref[i, :RANK, :] for i in range(chunks)], axis=1)
    scale = jnp.concatenate([whole_ref[i, RANK : RANK + 1, :] for i in range(chunks)], axis=1)
    cols = b_ref.shape[1]
    out_ref[:, :cols] = product(split(raw * scale), split(b_ref[...]), NN)
    gram = lax.dot_general(
        raw, raw, NT, precision=lax.Precision.HIGHEST, preferred_element_type=jnp.float32
    )
    out_ref[:, cols:] = jnp.concatenate([gram, jnp.zeros((RANK, LANES - RANK), jnp.float32)], axis=1)


def inverse_factor(gram):
    sub = lax.broadcasted_iota(jnp.int32, (RANK, LANES), 0)
    lane = lax.broadcasted_iota(jnp.int32, (RANK, LANES), 1)
    diag = jnp.where(sub == lane, gram, 0.0)
    down = lax.rsqrt(jnp.sum(diag, axis=1, keepdims=True))
    across = lax.rsqrt(jnp.where(lane[:1] < RANK, jnp.sum(diag, axis=0, keepdims=True), 1.0))
    full = jnp.where(lane < RANK, gram * across, (lane == RANK + sub).astype(jnp.float32)) * down
    work = [full[8 * b : 8 * b + 8] for b in range(RANK // 8)]
    sub = lax.broadcasted_iota(jnp.int32, (8, LANES), 0)
    wide = (8, LANES)

    def spread_row(value, s):
        return jnp.broadcast_to(value[s : s + 1, :], wide)

    out = []
    for at in range(RANK // 8):
        below = range(at, RANK // 8)
        columns = {
            i: [jnp.broadcast_to(work[i][:, 8 * at + j : 8 * at + j + 1], wide) for j in range(8)] for i in below
        }
        done = None
        for s in range(0, 8, 2):
            mine = columns[at]
            a, b, c = spread_row(mine[s], s), spread_row(mine[s], s + 1), spread_row(mine[s + 1], s + 1)
            top, low = spread_row(work[at], s), spread_row(work[at], s + 1)
            det = a * c - b * b
            inv = 1.0 / det
            ca, cb, cc = a * inv, b * inv, c * inv
            upper, lower = cc * top - cb * low, ca * low - cb * top
            pairs = {}
            for j in range(s + 2, 8):
                tj, lj = spread_row(mine[j], s), spread_row(mine[j], s + 1)
                pairs[j] = (cc * tj - cb * lj, ca * lj - cb * tj)
            for i in below:
                first, second = columns[i][s], columns[i][s + 1]
                if i == at:
                    first = jnp.where(sub > s + 1, first, 0.0)
                    second = jnp.where(sub > s + 1, second, 0.0)
                for j, (uj, wj) in pairs.items():
                    columns[i][j] = columns[i][j] - (first * uj + second * wj)
                work[i] = work[i] - (first * upper + second * lower)
            ratio = 1.0 / a
            one = top * lax.rsqrt(a)
            two = (low - (b * ratio) * top) * lax.rsqrt(det * ratio)
            done = one if s == 0 else jnp.where(sub == s, one, done)
            done = jnp.where(sub == s + 1, two, done)
        out.append(done)
    return jnp.concatenate(out, axis=0)[:, RANK:]


def finish_kernel(both_ref, whole_ref, scale_ref, left_ref, right_ref):
    chunks = whole_ref.shape[0]
    cols = scale_ref.shape[1]
    inverse = split(inverse_factor(both_ref[:, cols:]))
    for i in range(chunks):
        left_ref[:, LANES * i : LANES * (i + 1)] = product(inverse, split(whole_ref[i, :RANK, :]), NN)
    right_ref[...] = product(inverse, split(both_ref[:, :cols] * scale_ref[...]), NN)


def groups(*order):
    sizes = dict(zip("xzc", GRID))
    fixed = [name for name in "xzc" if name not in order]

    def lists(names):
        return itertools.product(*[range(sizes[name]) for name in names])

    def index(at):
        return (at["x"] * sizes["z"] + (at["z"] + FIRST_Z) % sizes["z"]) * sizes["c"] + at["c"]

    return [[index(dict(zip(fixed, f)) | dict(zip(order, m))) for m in lists(order)] for f in lists(fixed)]


def exchange(x, axis, members):
    return lax.all_to_all(x, axis, 0, 0, axis_index_groups=members)


def spread(x, axis, members):
    return exchange(jnp.broadcast_to(x[None], (len(members[0]),) + x.shape), axis, members)


def body(behaviour, panel):
    feats = lax.axis_size("feat")
    rows, cols = behaviour.shape
    every, near, far = groups("x", "z", "c"), groups("x", "c"), groups("z")
    feat = [[(i + FIRST_Y) % feats for i in range(feats)]]
    f32 = jnp.float32
    shape = jax.ShapeDtypeStruct

    sums = call(
        column_kernel, shape((len(every[0]), cols // LANES, LANES), f32), (behaviour,), "columns", rows * cols, 4 * rows * cols
    )
    sums = exchange(sums, "cand", every)
    part, col_scale = call(
        project_kernel,
        (shape((feats, PAD, rows // feats), f32), shape((1, cols), f32)),
        (behaviour, panel.T, sums),
        "project",
        6 * rows * cols * PAD,
        4 * rows * cols,
    )
    part = exchange(part, "feat", feat)
    mine = call(
        normalise_kernel, shape(part.shape, f32), (part,), "normalise", part.size, 8 * part.size
    )
    whole = exchange(mine, "feat", feat)
    both = call(
        reduce_kernel, shape((RANK, cols + LANES), f32), (behaviour, whole), "reduce", 6 * rows * cols * RANK, 4 * rows * cols
    )
    both = exchange(both.reshape(len(near[0]), -1, cols + LANES), "cand", near)
    line = jnp.sum(both, axis=0)
    line = jnp.sum(spread(line, "cand", far), axis=0)
    both = spread(line, "cand", near).reshape(RANK, cols + LANES)
    left, right = call(
        finish_kernel,
        (shape((RANK, rows), f32), shape((RANK, cols), f32)),
        (both, whole, col_scale),
        "finish",
        6 * RANK * RANK * (rows + cols),
        8 * RANK * (rows + cols),
    )
    return (left.T, right.T)


def solution(mesh):
    assert GRID[0] * GRID[1] * GRID[2] == mesh.shape["cand"]
    in_specs = (P("cand", "feat"), P("feat", None))
    out_specs = (P("cand", None), P("feat", None))
    return jax.shard_map(body, mesh=mesh, in_specs=in_specs, out_specs=out_specs, check_vma=False)
```

```python
import itertools

import jax
import jax.numpy as jnp
from jax import lax
from jax.experimental import pallas as pl
from jax.experimental.pallas import tpu as pltpu
from jax.sharding import PartitionSpec as P

RANK = 64
PAD = RANK + 8
LANES = 128
GRID = (4, 8, 2)
FIRST_X, FIRST_Y, FIRST_Z = 2, 6, 6
NT = (((1,), (1,)), ((), ()))
NN = (((1,), (0,)), ((), ()))


def split(a):
    high = a.astype(jnp.bfloat16)
    low = (a - high.astype(jnp.float32)).astype(jnp.bfloat16)
    return high, low


def product(a, b, dims):
    m = a[0].shape[0]
    stacked = jnp.concatenate([a[0], a[1]], axis=0)
    full = lax.dot_general(stacked, b[0], dims, preferred_element_type=jnp.float32)
    rest = lax.dot_general(a[0], b[1], dims, preferred_element_type=jnp.float32)
    return full[:m] + (full[m:] + rest)


def call(kernel, out_shape, operands, name, flops, nbytes):
    return pl.pallas_call(
        kernel,
        out_shape=out_shape,
        name=name,
        in_specs=[pl.BlockSpec(memory_space=pltpu.VMEM)] * len(operands),
        out_specs=jax.tree.map(lambda _: pl.BlockSpec(memory_space=pltpu.VMEM), out_shape),
        cost_estimate=pl.CostEstimate(flops=flops, bytes_accessed=nbytes, transcendentals=0),
        compiler_params=pltpu.CompilerParams(vmem_limit_bytes=24 << 20),
    )(*operands)


def column_kernel(b_ref, out_ref):
    copies, parts, _ = out_ref.shape
    sums = jnp.sum(b_ref[...], axis=0, keepdims=True)
    rows = jnp.concatenate([sums[:, LANES * i : LANES * (i + 1)] for i in range(parts)], axis=0)
    out_ref[...] = jnp.broadcast_to(rows[None], out_ref.shape)


def project_kernel(b_ref, panel_ref, sums_ref, out_ref, scale_ref):
    parts = sums_ref.shape[1]
    deg = jnp.sum(sums_ref[...], axis=0)
    deg = jnp.concatenate([deg[i : i + 1] for i in range(parts)], axis=1)
    scale = lax.rsqrt(deg)
    scale_ref[...] = scale
    ones = jnp.ones((PAD - RANK, deg.shape[1]), jnp.float32)
    left = split(jnp.concatenate([panel_ref[...] * scale, ones], axis=0))
    for i in range(out_ref.shape[0]):
        out_ref[i] = product(left, split(b_ref[LANES * i : LANES * (i + 1), :]), NT)


def normalise_kernel(parts_ref, out_ref):
    total = jnp.sum(parts_ref[...], axis=0)
    scale = lax.rsqrt(total[RANK:])
    out = jnp.concatenate([total[:RANK] * scale[:1], scale], axis=0)
    out_ref[...] = jnp.broadcast_to(out[None], out_ref.shape)


def reduce_kernel(b_ref, whole_ref, out_ref):
    chunks = whole_ref.shape[0]
    raw = jnp.concatenate([whole_ref[i, :RANK, :] for i in range(chunks)], axis=1)
    scale = jnp.concatenate([whole_ref[i, RANK : RANK + 1, :] for i in range(chunks)], axis=1)
    cols = b_ref.shape[1]
    out_ref[:, :cols] = product(split(raw * scale), split(b_ref[...]), NN)
    gram = lax.dot_general(
        raw, raw, NT, precision=lax.Precision.HIGHEST, preferred_element_type=jnp.float32
    )
    out_ref[:, cols:] = jnp.concatenate([gram, jnp.zeros((RANK, LANES - RANK), jnp.float32)], axis=1)


def inverse_factor(gram):
    sub = lax.broadcasted_iota(jnp.int32, (RANK, LANES), 0)
    lane = lax.broadcasted_iota(jnp.int32, (RANK, LANES), 1)
    diag = jnp.where(sub == lane, gram, 0.0)
    down = lax.rsqrt(jnp.sum(diag, axis=1, keepdims=True))
    across = lax.rsqrt(jnp.where(lane[:1] < RANK, jnp.sum(diag, axis=0, keepdims=True), 1.0))
    full = jnp.where(lane < RANK, gram * across, (lane == RANK + sub).astype(jnp.float32)) * down
    work = [full[8 * b : 8 * b + 8] for b in range(RANK // 8)]
    sub = lax.broadcasted_iota(jnp.int32, (8, LANES), 0)
    wide = (8, LANES)

    def spread_row(value, s):
        return jnp.broadcast_to(value[s : s + 1, :], wide)

    def lanes_of(i, start):
        return [jnp.broadcast_to(work[i][:, start + j : start + j + 1], wide) for j in range(8)]

    out = []
    blocks = RANK // 8
    mine = lanes_of(0, 0)
    for at in range(blocks):
        below = range(at + 1, blocks)
        columns = {i: lanes_of(i, 8 * at) for i in below}
        ahead = lanes_of(at + 1, 8 * at + 8) if below else []
        done = None
        for s in range(0, 8, 2):
            a, b, c = spread_row(mine[s], s), spread_row(mine[s], s + 1), spread_row(mine[s + 1], s + 1)
            top, low = spread_row(work[at], s), spread_row(work[at], s + 1)
            det = a * c - b * b
            inv = 1.0 / det
            ca, cb, cc = a * inv, b * inv, c * inv
            upper, lower = cc * top - cb * low, ca * low - cb * top
            first = jnp.where(sub > s + 1, mine[s], 0.0)
            second = jnp.where(sub > s + 1, mine[s + 1], 0.0)
            pairs = {}
            for j in range(s + 2, 8):
                tj, lj = spread_row(mine[s], j), spread_row(mine[s + 1], j)
                uj, wj = cc * tj - cb * lj, ca * lj - cb * tj
                pairs[j] = uj, wj
                mine[j] = mine[j] - (first * uj + second * wj)
            work[at] = work[at] - (first * upper + second * lower)
            if below:
                first, second = columns[at + 1][s], columns[at + 1][s + 1]
                for j in range(8):
                    tj, lj = spread_row(first, j), spread_row(second, j)
                    ahead[j] = ahead[j] - (first * (cc * tj - cb * lj) + second * (ca * lj - cb * tj))
            for i in below:
                first, second = columns[i][s], columns[i][s + 1]
                for j, (uj, wj) in pairs.items():
                    columns[i][j] = columns[i][j] - (first * uj + second * wj)
                work[i] = work[i] - (first * upper + second * lower)
            ratio = 1.0 / a
            one = top * lax.rsqrt(a)
            two = (low - (b * ratio) * top) * lax.rsqrt(det * ratio)
            done = one if s == 0 else jnp.where(sub == s, one, done)
            done = jnp.where(sub == s + 1, two, done)
        out.append(done)
        mine = ahead
    return jnp.concatenate(out, axis=0)[:, RANK:]


def finish_kernel(both_ref, whole_ref, scale_ref, left_ref, right_ref):
    chunks = whole_ref.shape[0]
    cols = scale_ref.shape[1]
    inverse = inverse_factor(both_ref[:, cols:])
    sides = [whole_ref[i, :RANK, :] for i in range(chunks)] + [both_ref[:, :cols] * scale_ref[...]]
    solved = lax.dot_general(
        inverse, jnp.concatenate(sides, axis=1), NN, precision=lax.Precision.HIGHEST, preferred_element_type=jnp.float32
    )
    left_ref[...] = solved[:, : chunks * LANES]
    right_ref[...] = solved[:, chunks * LANES :]


def groups(*order):
    sizes = dict(zip("xzc", GRID))
    fixed = [name for name in "xzc" if name not in order]

    def lists(names):
        return itertools.product(*[range(sizes[name]) for name in names])

    def index(at):
        x, z = (at["x"] + FIRST_X) % sizes["x"], (at["z"] + FIRST_Z) % sizes["z"]
        return (x * sizes["z"] + z) * sizes["c"] + at["c"]

    return [[index(dict(zip(fixed, f)) | dict(zip(order, m))) for m in lists(order)] for f in lists(fixed)]


def exchange(x, axis, members):
    return lax.all_to_all(x, axis, 0, 0, axis_index_groups=members)


def spread(x, axis, members):
    return exchange(jnp.broadcast_to(x[None], (len(members[0]),) + x.shape), axis, members)


def body(behaviour, panel):
    feats = lax.axis_size("feat")
    rows, cols = behaviour.shape
    every, near, far = groups("x", "z", "c"), groups("x", "c"), groups("z")
    feat = [[(i + FIRST_Y) % feats for i in range(feats)]]
    f32 = jnp.float32
    shape = jax.ShapeDtypeStruct

    sums = call(
        column_kernel, shape((len(every[0]), cols // LANES, LANES), f32), (behaviour,), "columns", rows * cols, 4 * rows * cols
    )
    sums = exchange(sums, "cand", every)
    part, col_scale = call(
        project_kernel,
        (shape((feats, PAD, rows // feats), f32), shape((1, cols), f32)),
        (behaviour, panel.T, sums),
        "project",
        6 * rows * cols * PAD,
        4 * rows * cols,
    )
    part = exchange(part, "feat", feat)
    mine = call(
        normalise_kernel, shape(part.shape, f32), (part,), "normalise", part.size, 8 * part.size
    )
    whole = exchange(mine, "feat", feat)
    both = call(
        reduce_kernel, shape((RANK, cols + LANES), f32), (behaviour, whole), "reduce", 6 * rows * cols * RANK, 4 * rows * cols
    )
    both = exchange(both.reshape(len(near[0]), -1, cols + LANES), "cand", near)
    line = jnp.sum(both, axis=0)
    line = jnp.sum(spread(line, "cand", far), axis=0)
    both = spread(line, "cand", near).reshape(RANK, cols + LANES)
    left, right = call(
        finish_kernel,
        (shape((RANK, rows), f32), shape((RANK, cols), f32)),
        (both, whole, col_scale),
        "finish",
        6 * RANK * RANK * (rows + cols),
        8 * RANK * (rows + cols),
    )
    return (left.T, right.T)


def solution(mesh):
    assert GRID[0] * GRID[1] * GRID[2] == mesh.shape["cand"]
    in_specs = (P("cand", "feat"), P("feat", None))
    out_specs = (P("cand", None), P("feat", None))
    return jax.shard_map(body, mesh=mesh, in_specs=in_specs, out_specs=out_specs, check_vma=False)
```

```python
import itertools

import jax
import jax.numpy as jnp
from jax import lax
from jax.experimental import pallas as pl
from jax.experimental.pallas import tpu as pltpu
from jax.sharding import PartitionSpec as P

RANK = 64
PAD = RANK + 8
LANES = 128
GRID = (4, 8, 2)
FIRST_X, FIRST_Y, FIRST_Z = 2, 6, 6
NT = (((1,), (1,)), ((), ()))
NN = (((1,), (0,)), ((), ()))


def split(a):
    high = a.astype(jnp.bfloat16)
    low = (a - high.astype(jnp.float32)).astype(jnp.bfloat16)
    return high, low


def product(a, b, dims):
    m = a[0].shape[0]
    stacked = jnp.concatenate([a[0], a[1]], axis=0)
    full = lax.dot_general(stacked, b[0], dims, preferred_element_type=jnp.float32)
    rest = lax.dot_general(a[0], b[1], dims, preferred_element_type=jnp.float32)
    return full[:m] + (full[m:] + rest)


def call(kernel, out_shape, operands, name, flops, nbytes):
    return pl.pallas_call(
        kernel,
        out_shape=out_shape,
        name=name,
        in_specs=[pl.BlockSpec(memory_space=pltpu.VMEM)] * len(operands),
        out_specs=jax.tree.map(lambda _: pl.BlockSpec(memory_space=pltpu.VMEM), out_shape),
        cost_estimate=pl.CostEstimate(flops=flops, bytes_accessed=nbytes, transcendentals=0),
        compiler_params=pltpu.CompilerParams(vmem_limit_bytes=24 << 20),
    )(*operands)


def column_kernel(b_ref, out_ref):
    copies, parts, _ = out_ref.shape
    sums = jnp.sum(b_ref[...], axis=0, keepdims=True)
    rows = jnp.concatenate([sums[:, LANES * i : LANES * (i + 1)] for i in range(parts)], axis=0)
    out_ref[...] = jnp.broadcast_to(rows[None], out_ref.shape)


def project_kernel(b_ref, panel_ref, sums_ref, out_ref, rows_ref, scale_ref):
    parts = sums_ref.shape[1]
    deg = jnp.sum(sums_ref[...], axis=0)
    deg = jnp.concatenate([deg[i : i + 1] for i in range(parts)], axis=1)
    scale = lax.rsqrt(deg)
    scale_ref[...] = scale
    ones = jnp.ones((8, deg.shape[1]), jnp.float32)
    left = split(jnp.concatenate([panel_ref[...] * scale, ones], axis=0))
    for i in range(out_ref.shape[0]):
        piece = product(left, split(b_ref[LANES * i : LANES * (i + 1), :]), NT)
        out_ref[i] = piece[:RANK]
        rows_ref[i : i + 1, :] = piece[RANK : RANK + 1]


def share_kernel(parts_ref, rows_ref, out_ref):
    out = jnp.concatenate([jnp.sum(parts_ref[...], axis=0), rows_ref[...]], axis=0)
    out_ref[...] = jnp.broadcast_to(out[None], out_ref.shape)


def reduce_kernel(b_ref, whole_ref, out_ref, raw_ref):
    chunks = whole_ref.shape[0]
    scale = lax.rsqrt(jnp.sum(whole_ref[:, RANK:, :], axis=0))
    scale = jnp.concatenate([scale[i : i + 1] for i in range(chunks)], axis=1)
    raw = jnp.concatenate([whole_ref[i, :RANK, :] for i in range(chunks)], axis=1) * scale
    raw_ref[...] = raw
    cols = b_ref.shape[1]
    out_ref[:, :cols] = product(split(raw * scale), split(b_ref[...]), NN)
    gram = lax.dot_general(
        raw, raw, NT, precision=lax.Precision.HIGHEST, preferred_element_type=jnp.float32
    )
    out_ref[:, cols:] = jnp.concatenate([gram, jnp.zeros((RANK, LANES - RANK), jnp.float32)], axis=1)


def inverse_factor(gram):
    sub = lax.broadcasted_iota(jnp.int32, (RANK, LANES), 0)
    lane = lax.broadcasted_iota(jnp.int32, (RANK, LANES), 1)
    diag = jnp.where(sub == lane, gram, 0.0)
    down = lax.rsqrt(jnp.sum(diag, axis=1, keepdims=True))
    across = lax.rsqrt(jnp.where(lane[:1] < RANK, jnp.sum(diag, axis=0, keepdims=True), 1.0))
    full = jnp.where(lane < RANK, gram * across, (lane == RANK + sub).astype(jnp.float32)) * down
    work = [full[8 * b : 8 * b + 8] for b in range(RANK // 8)]
    sub = lax.broadcasted_iota(jnp.int32, (8, LANES), 0)
    wide = (8, LANES)

    def spread_row(value, s):
        return jnp.broadcast_to(value[s : s + 1, :], wide)

    def lanes_of(i, start):
        return [jnp.broadcast_to(work[i][:, start + j : start + j + 1], wide) for j in range(8)]

    out = []
    blocks = RANK // 8
    mine = lanes_of(0, 0)
    for at in range(blocks):
        below = range(at + 1, blocks)
        columns = {i: lanes_of(i, 8 * at) for i in below}
        ahead = lanes_of(at + 1, 8 * at + 8) if below else []
        done = None
        for s in range(0, 8, 2):
            a, b, c = spread_row(mine[s], s), spread_row(mine[s], s + 1), spread_row(mine[s + 1], s + 1)
            top, low = spread_row(work[at], s), spread_row(work[at], s + 1)
            det = a * c - b * b
            inv = 1.0 / det
            ca, cb, cc = a * inv, b * inv, c * inv
            upper, lower = cc * top - cb * low, ca * low - cb * top
            first = jnp.where(sub > s + 1, mine[s], 0.0)
            second = jnp.where(sub > s + 1, mine[s + 1], 0.0)
            pairs = {}
            for j in range(s + 2, 8):
                tj, lj = spread_row(mine[s], j), spread_row(mine[s + 1], j)
                uj, wj = cc * tj - cb * lj, ca * lj - cb * tj
                pairs[j] = uj, wj
                mine[j] = mine[j] - (first * uj + second * wj)
            work[at] = work[at] - (first * upper + second * lower)
            if below:
                first, second = columns[at + 1][s], columns[at + 1][s + 1]
                for j in range(8):
                    tj, lj = spread_row(first, j), spread_row(second, j)
                    ahead[j] = ahead[j] - (first * (cc * tj - cb * lj) + second * (ca * lj - cb * tj))
            for i in below:
                first, second = columns[i][s], columns[i][s + 1]
                for j, (uj, wj) in pairs.items():
                    columns[i][j] = columns[i][j] - (first * uj + second * wj)
                work[i] = work[i] - (first * upper + second * lower)
            ratio = 1.0 / a
            one = top * lax.rsqrt(a)
            two = (low - (b * ratio) * top) * lax.rsqrt(det * ratio)
            done = one if s == 0 else jnp.where(sub == s, one, done)
            done = jnp.where(sub == s + 1, two, done)
        out.append(done)
        mine = ahead
    return jnp.concatenate(out, axis=0)[:, RANK:]


def finish_kernel(both_ref, raw_ref, scale_ref, left_ref, right_ref):
    rows, cols = raw_ref.shape[1], scale_ref.shape[1]
    inverse = inverse_factor(both_ref[:, cols:])
    sides = jnp.concatenate([raw_ref[...], both_ref[:, :cols] * scale_ref[...]], axis=1)
    solved = lax.dot_general(
        inverse, sides, NN, precision=lax.Precision.HIGHEST, preferred_element_type=jnp.float32
    )
    left_ref[...] = solved[:, :rows]
    right_ref[...] = solved[:, rows:]


def groups(*order):
    sizes = dict(zip("xzc", GRID))
    fixed = [name for name in "xzc" if name not in order]

    def lists(names):
        return itertools.product(*[range(sizes[name]) for name in names])

    def index(at):
        x, z = (at["x"] + FIRST_X) % sizes["x"], (at["z"] + FIRST_Z) % sizes["z"]
        return (x * sizes["z"] + z) * sizes["c"] + 1 - at["c"]

    return [[index(dict(zip(fixed, f)) | dict(zip(order, m))) for m in lists(order)] for f in lists(fixed)]


def exchange(x, axis, members):
    return lax.all_to_all(x, axis, 0, 0, axis_index_groups=members)


def spread(x, axis, members):
    return exchange(jnp.broadcast_to(x[None], (len(members[0]),) + x.shape), axis, members)


def body(behaviour, panel):
    feats = lax.axis_size("feat")
    rows, cols = behaviour.shape
    assert rows == feats * LANES and feats == 8
    every, near, far = groups("x", "z", "c"), groups("x", "c"), groups("z")
    feat = [[(i + FIRST_Y) % feats for i in range(feats)]]
    f32 = jnp.float32
    shape = jax.ShapeDtypeStruct

    sums = call(
        column_kernel, shape((len(every[0]), cols // LANES, LANES), f32), (behaviour,), "columns", rows * cols, 4 * rows * cols
    )
    sums = exchange(sums, "cand", every)
    part, row_sums, col_scale = call(
        project_kernel,
        (shape((feats, RANK, LANES), f32), shape((feats, LANES), f32), shape((1, cols), f32)),
        (behaviour, panel.T, sums),
        "project",
        6 * rows * cols * PAD,
        4 * rows * cols,
    )
    part = exchange(part, "feat", feat)
    share = call(
        share_kernel, shape((feats, PAD, LANES), f32), (part, row_sums), "share", part.size, 8 * part.size
    )
    whole = exchange(share, "feat", feat)
    both, raw = call(
        reduce_kernel,
        (shape((RANK, cols + LANES), f32), shape((RANK, rows), f32)),
        (behaviour, whole),
        "reduce",
        6 * rows * cols * RANK,
        4 * rows * cols,
    )
    both = exchange(both.reshape(len(near[0]), -1, cols + LANES), "cand", near)
    line = jnp.sum(both, axis=0)
    line = jnp.sum(spread(line, "cand", far), axis=0)
    both = spread(line, "cand", near).reshape(RANK, cols + LANES)
    left, right = call(
        finish_kernel,
        (shape((RANK, rows), f32), shape((RANK, cols), f32)),
        (both, raw, col_scale),
        "finish",
        6 * RANK * RANK * (rows + cols),
        8 * RANK * (rows + cols),
    )
    return (left.T, right.T)


def solution(mesh):
    assert GRID[0] * GRID[1] * GRID[2] == mesh.shape["cand"]
    in_specs = (P("cand", "feat"), P("feat", None))
    out_specs = (P("cand", None), P("feat", None))
    return jax.shard_map(body, mesh=mesh, in_specs=in_specs, out_specs=out_specs, check_vma=False)
```

```python
import itertools

import jax
import jax.numpy as jnp
from jax import lax
from jax.experimental import pallas as pl
from jax.experimental.pallas import tpu as pltpu
from jax.sharding import PartitionSpec as P

RANK = 64
PAD = RANK + 8
LANES = 128
GRID = (4, 8, 2)
FIRST_X, FIRST_Y, FIRST_Z = 2, 5, 6
NT = (((1,), (1,)), ((), ()))
NN = (((1,), (0,)), ((), ()))


def split(a):
    high = a.astype(jnp.bfloat16)
    low = (a - high.astype(jnp.float32)).astype(jnp.bfloat16)
    return high, low


def product(a, b, dims):
    m = a[0].shape[0]
    stacked = jnp.concatenate([a[0], a[1]], axis=0)
    full = lax.dot_general(stacked, b[0], dims, preferred_element_type=jnp.float32)
    rest = lax.dot_general(a[0], b[1], dims, preferred_element_type=jnp.float32)
    return full[:m] + (full[m:] + rest)


def call(kernel, out_shape, operands, name, flops, nbytes):
    return pl.pallas_call(
        kernel,
        out_shape=out_shape,
        name=name,
        in_specs=[pl.BlockSpec(memory_space=pltpu.VMEM)] * len(operands),
        out_specs=jax.tree.map(lambda _: pl.BlockSpec(memory_space=pltpu.VMEM), out_shape),
        cost_estimate=pl.CostEstimate(flops=flops, bytes_accessed=nbytes, transcendentals=0),
        compiler_params=pltpu.CompilerParams(vmem_limit_bytes=24 << 20),
    )(*operands)


def column_kernel(b_ref, out_ref):
    copies, parts, _ = out_ref.shape
    sums = jnp.sum(b_ref[...], axis=0, keepdims=True)
    rows = jnp.concatenate([sums[:, LANES * i : LANES * (i + 1)] for i in range(parts)], axis=0)
    out_ref[...] = jnp.broadcast_to(rows[None], out_ref.shape)


def project_kernel(b_ref, panel_ref, sums_ref, out_ref, rows_ref, scale_ref):
    parts = sums_ref.shape[1]
    deg = jnp.sum(sums_ref[...], axis=0)
    deg = jnp.concatenate([deg[i : i + 1] for i in range(parts)], axis=1)
    scale = lax.rsqrt(deg)
    scale_ref[...] = scale
    ones = jnp.ones((8, deg.shape[1]), jnp.float32)
    left = split(jnp.concatenate([panel_ref[...] * scale, ones], axis=0))
    for i in range(out_ref.shape[0]):
        piece = product(left, split(b_ref[LANES * i : LANES * (i + 1), :]), NT)
        out_ref[i] = piece[:RANK]
        rows_ref[i : i + 1, :] = piece[RANK : RANK + 1]


def share_kernel(parts_ref, rows_ref, out_ref):
    out = jnp.concatenate([jnp.sum(parts_ref[...], axis=0), rows_ref[...]], axis=0)
    out_ref[...] = jnp.broadcast_to(out[None], out_ref.shape)


def reduce_kernel(b_ref, whole_ref, out_ref, raw_ref):
    chunks = whole_ref.shape[0]
    scale = lax.rsqrt(jnp.sum(whole_ref[:, RANK:, :], axis=0))
    scale = jnp.concatenate([scale[i : i + 1] for i in range(chunks)], axis=1)
    raw = jnp.concatenate([whole_ref[i, :RANK, :] for i in range(chunks)], axis=1) * scale
    raw_ref[...] = raw
    cols = b_ref.shape[1]
    out_ref[:, :cols] = product(split(raw * scale), split(b_ref[...]), NN)
    gram = lax.dot_general(
        raw, raw, NT, precision=lax.Precision.HIGHEST, preferred_element_type=jnp.float32
    )
    out_ref[:, cols:] = jnp.concatenate([gram, jnp.zeros((RANK, LANES - RANK), jnp.float32)], axis=1)


def inverse_factor(gram):
    sub = lax.broadcasted_iota(jnp.int32, (RANK, LANES), 0)
    lane = lax.broadcasted_iota(jnp.int32, (RANK, LANES), 1)
    diag = jnp.where(sub == lane, gram, 0.0)
    down = lax.rsqrt(jnp.sum(diag, axis=1, keepdims=True))
    across = lax.rsqrt(jnp.where(lane[:1] < RANK, jnp.sum(diag, axis=0, keepdims=True), 1.0))
    full = jnp.where(lane < RANK, gram * across, (lane == RANK + sub).astype(jnp.float32)) * down
    work = [full[8 * b : 8 * b + 8] for b in range(RANK // 8)]
    sub = lax.broadcasted_iota(jnp.int32, (8, LANES), 0)
    wide = (8, LANES)

    def spread_row(value, s):
        return jnp.broadcast_to(value[s : s + 1, :], wide)

    def lanes_of(i, start):
        return [jnp.broadcast_to(work[i][:, start + j : start + j + 1], wide) for j in range(8)]

    out = []
    blocks = RANK // 8
    mine = lanes_of(0, 0)
    for at in range(blocks):
        below = range(at + 1, blocks)
        columns = {i: lanes_of(i, 8 * at) for i in below}
        ahead = lanes_of(at + 1, 8 * at + 8) if below else []
        done = None
        for s in range(0, 8, 2):
            a, b, c = spread_row(mine[s], s), spread_row(mine[s], s + 1), spread_row(mine[s + 1], s + 1)
            top, low = spread_row(work[at], s), spread_row(work[at], s + 1)
            det = a * c - b * b
            inv = 1.0 / det
            ca, cb, cc = a * inv, b * inv, c * inv
            upper, lower = cc * top - cb * low, ca * low - cb * top
            first = jnp.where(sub > s + 1, mine[s], 0.0)
            second = jnp.where(sub > s + 1, mine[s + 1], 0.0)
            pairs = {}
            for j in range(s + 2, 8):
                tj, lj = spread_row(mine[s], j), spread_row(mine[s + 1], j)
                uj, wj = cc * tj - cb * lj, ca * lj - cb * tj
                pairs[j] = uj, wj
                mine[j] = mine[j] - (first * uj + second * wj)
            work[at] = work[at] - (first * upper + second * lower)
            if below:
                first, second = columns[at + 1][s], columns[at + 1][s + 1]
                for j in range(8):
                    tj, lj = spread_row(first, j), spread_row(second, j)
                    ahead[j] = ahead[j] - (first * (cc * tj - cb * lj) + second * (ca * lj - cb * tj))
            for i in below:
                first, second = columns[i][s], columns[i][s + 1]
                for j, (uj, wj) in pairs.items():
                    columns[i][j] = columns[i][j] - (first * uj + second * wj)
                work[i] = work[i] - (first * upper + second * lower)
            ratio = 1.0 / a
            one = top * lax.rsqrt(a)
            two = (low - (b * ratio) * top) * lax.rsqrt(det * ratio)
            done = one if s == 0 else jnp.where(sub == s, one, done)
            done = jnp.where(sub == s + 1, two, done)
        out.append(done)
        mine = ahead
    return jnp.concatenate(out, axis=0)[:, RANK:]


def finish_kernel(both_ref, raw_ref, scale_ref, left_ref, right_ref):
    rows, cols = raw_ref.shape[1], scale_ref.shape[1]
    inverse = inverse_factor(both_ref[:, cols:])
    sides = jnp.concatenate([raw_ref[...], both_ref[:, :cols] * scale_ref[...]], axis=1)
    solved = lax.dot_general(
        inverse, sides, NN, precision=lax.Precision.HIGHEST, preferred_element_type=jnp.float32
    )
    left_ref[...] = solved[:, :rows]
    right_ref[...] = solved[:, rows:]


def groups(*order):
    sizes = dict(zip("xzc", GRID))
    fixed = [name for name in "xzc" if name not in order]

    def lists(names):
        return itertools.product(*[range(sizes[name]) for name in names])

    def index(at):
        x, z = (at["x"] + FIRST_X) % sizes["x"], (at["z"] + FIRST_Z) % sizes["z"]
        return (x * sizes["z"] + z) * sizes["c"] + 1 - at["c"]

    return [[index(dict(zip(fixed, f)) | dict(zip(order, m))) for m in lists(order)] for f in lists(fixed)]


def exchange(x, axis, members):
    return lax.all_to_all(x, axis, 0, 0, axis_index_groups=members)


def spread(x, axis, members):
    return exchange(jnp.broadcast_to(x[None], (len(members[0]),) + x.shape), axis, members)


def body(behaviour, panel):
    feats = lax.axis_size("feat")
    rows, cols = behaviour.shape
    assert rows == feats * LANES and feats == 8
    every, near, far = groups("x", "z", "c"), groups("x", "c"), groups("z")
    feat = [[(i + FIRST_Y) % feats for i in range(feats)]]
    f32 = jnp.float32
    shape = jax.ShapeDtypeStruct

    sums = call(
        column_kernel, shape((len(every[0]), cols // LANES, LANES), f32), (behaviour,), "columns", rows * cols, 4 * rows * cols
    )
    sums = exchange(sums, "cand", every)
    part, row_sums, col_scale = call(
        project_kernel,
        (shape((feats, RANK, LANES), f32), shape((feats, LANES), f32), shape((1, cols), f32)),
        (behaviour, panel.T, sums),
        "project",
        6 * rows * cols * PAD,
        4 * rows * cols,
    )
    part = exchange(part, "feat", feat)
    share = call(
        share_kernel, shape((feats, PAD, LANES), f32), (part, row_sums), "share", part.size, 8 * part.size
    )
    whole = exchange(share, "feat", feat)
    both, raw = call(
        reduce_kernel,
        (shape((RANK, cols + LANES), f32), shape((RANK, rows), f32)),
        (behaviour, whole),
        "reduce",
        6 * rows * cols * RANK,
        4 * rows * cols,
    )
    both = exchange(both.reshape(len(near[0]), -1, cols + LANES), "cand", near)
    line = jnp.sum(both, axis=0)
    line = jnp.sum(spread(line, "cand", far), axis=0)
    both = spread(line, "cand", near).reshape(RANK, cols + LANES)
    left, right = call(
        finish_kernel,
        (shape((RANK, rows), f32), shape((RANK, cols), f32)),
        (both, raw, col_scale),
        "finish",
        6 * RANK * RANK * (rows + cols),
        8 * RANK * (rows + cols),
    )
    return (left.T, right.T)


def solution(mesh):
    assert GRID[0] * GRID[1] * GRID[2] == mesh.shape["cand"]
    in_specs = (P("cand", "feat"), P("feat", None))
    out_specs = (P("cand", None), P("feat", None))
    return jax.shard_map(body, mesh=mesh, in_specs=in_specs, out_specs=out_specs, check_vma=False)
```

```python
import itertools

import jax
import jax.numpy as jnp
from jax import lax
from jax.experimental import pallas as pl
from jax.experimental.pallas import tpu as pltpu
from jax.sharding import PartitionSpec as P

RANK = 64
PAD = RANK + 8
LANES = 128
GRID = (4, 8, 2)
FIRST_X, FIRST_Y, FIRST_Z = 2, 5, 6
NT = (((1,), (1,)), ((), ()))
NN = (((1,), (0,)), ((), ()))


def split(a):
    high = a.astype(jnp.bfloat16)
    low = (a - high.astype(jnp.float32)).astype(jnp.bfloat16)
    return high, low


def product(a, b, dims):
    m = a[0].shape[0]
    stacked = jnp.concatenate([a[0], a[1]], axis=0)
    full = lax.dot_general(stacked, b[0], dims, preferred_element_type=jnp.float32)
    rest = lax.dot_general(a[0], b[1], dims, preferred_element_type=jnp.float32)
    return full[:m] + (full[m:] + rest)


def call(kernel, out_shape, operands, name, flops, nbytes):
    return pl.pallas_call(
        kernel,
        out_shape=out_shape,
        name=name,
        in_specs=[pl.BlockSpec(memory_space=pltpu.VMEM)] * len(operands),
        out_specs=jax.tree.map(lambda _: pl.BlockSpec(memory_space=pltpu.VMEM), out_shape),
        cost_estimate=pl.CostEstimate(flops=flops, bytes_accessed=nbytes, transcendentals=0),
        compiler_params=pltpu.CompilerParams(vmem_limit_bytes=24 << 20),
    )(*operands)


def column_kernel(b_ref, out_ref):
    copies, parts, _ = out_ref.shape
    sums = jnp.sum(b_ref[...], axis=0, keepdims=True)
    rows = jnp.concatenate([sums[:, LANES * i : LANES * (i + 1)] for i in range(parts)], axis=0)
    out_ref[...] = jnp.broadcast_to(rows[None], out_ref.shape)


def project_kernel(b_ref, panel_ref, sums_ref, out_ref, rows_ref, scale_ref):
    parts = sums_ref.shape[1]
    deg = jnp.sum(sums_ref[...], axis=0)
    deg = jnp.concatenate([deg[i : i + 1] for i in range(parts)], axis=1)
    scale = lax.rsqrt(deg)
    scale_ref[...] = scale
    ones = jnp.ones((8, deg.shape[1]), jnp.float32)
    left = split(jnp.concatenate([panel_ref[...] * scale, ones], axis=0))
    for i in range(out_ref.shape[0]):
        piece = product(left, split(b_ref[LANES * i : LANES * (i + 1), :]), NT)
        out_ref[i] = piece[:RANK]
        rows_ref[i : i + 1, :] = piece[RANK : RANK + 1]


def share_kernel(parts_ref, rows_ref, out_ref):
    out = jnp.concatenate([jnp.sum(parts_ref[...], axis=0), rows_ref[...]], axis=0)
    out_ref[...] = jnp.broadcast_to(out[None], out_ref.shape)


def reduce_kernel(b_ref, whole_ref, out_ref, raw_ref):
    chunks = whole_ref.shape[0]
    scale = lax.rsqrt(jnp.sum(whole_ref[:, RANK:, :], axis=0))
    scale = jnp.concatenate([scale[i : i + 1] for i in range(chunks)], axis=1)
    raw = jnp.concatenate([whole_ref[i, :RANK, :] for i in range(chunks)], axis=1) * scale
    raw_ref[...] = raw
    cols = b_ref.shape[1]
    out_ref[:, :cols] = product(split(raw * scale), split(b_ref[...]), NN)
    gram = lax.dot_general(
        raw, raw, NT, precision=lax.Precision.HIGHEST, preferred_element_type=jnp.float32
    )
    out_ref[:, cols:] = jnp.concatenate([gram, jnp.zeros((RANK, LANES - RANK), jnp.float32)], axis=1)


def inverse_factor(gram):
    sub = lax.broadcasted_iota(jnp.int32, (RANK, LANES), 0)
    lane = lax.broadcasted_iota(jnp.int32, (RANK, LANES), 1)
    diag = jnp.where(sub == lane, gram, 0.0)
    down = lax.rsqrt(jnp.sum(diag, axis=1, keepdims=True))
    across = lax.rsqrt(jnp.where(lane[:1] < RANK, jnp.sum(diag, axis=0, keepdims=True), 1.0))
    full = jnp.where(lane < RANK, gram * across, (lane == RANK + sub).astype(jnp.float32)) * down
    work = [full[8 * b : 8 * b + 8] for b in range(RANK // 8)]
    sub = lax.broadcasted_iota(jnp.int32, (8, LANES), 0)
    wide = (8, LANES)

    def spread_row(value, s):
        return jnp.broadcast_to(value[s : s + 1, :], wide)

    def lanes_of(i, start):
        return [jnp.broadcast_to(work[i][:, start + j : start + j + 1], wide) for j in range(8)]

    out = []
    blocks = RANK // 8
    mine = lanes_of(0, 0)
    for at in range(blocks):
        below = range(at + 1, blocks)
        columns = {i: lanes_of(i, 8 * at) for i in below}
        ahead = lanes_of(at + 1, 8 * at + 8) if below else []
        done = None
        for s in range(0, 8, 2):
            a, b, c = spread_row(mine[s], s), spread_row(mine[s], s + 1), spread_row(mine[s + 1], s + 1)
            top, low = spread_row(work[at], s), spread_row(work[at], s + 1)
            det = a * c - b * b
            inv = 1.0 / det
            ca, cb, cc = a * inv, b * inv, c * inv
            upper, lower = cc * top - cb * low, ca * low - cb * top
            first = jnp.where(sub > s + 1, mine[s], 0.0)
            second = jnp.where(sub > s + 1, mine[s + 1], 0.0)
            pairs = {}
            for j in range(s + 2, 8):
                tj, lj = spread_row(mine[s], j), spread_row(mine[s + 1], j)
                uj, wj = cc * tj - cb * lj, ca * lj - cb * tj
                pairs[j] = uj, wj
                mine[j] = mine[j] - (first * uj + second * wj)
            work[at] = work[at] - (first * upper + second * lower)
            if below:
                first, second = columns[at + 1][s], columns[at + 1][s + 1]
                for j in range(8):
                    tj, lj = spread_row(first, j), spread_row(second, j)
                    ahead[j] = ahead[j] - (first * (cc * tj - cb * lj) + second * (ca * lj - cb * tj))
            for i in below:
                first, second = columns[i][s], columns[i][s + 1]
                for j, (uj, wj) in pairs.items():
                    columns[i][j] = columns[i][j] - (first * uj + second * wj)
                work[i] = work[i] - (first * upper + second * lower)
            ratio = 1.0 / a
            one = top * lax.rsqrt(a)
            two = (low - (b * ratio) * top) * lax.rsqrt(det * ratio)
            done = one if s == 0 else jnp.where(sub == s, one, done)
            done = jnp.where(sub == s + 1, two, done)
        out.append(done)
        mine = ahead
    return jnp.concatenate(out, axis=0)[:, RANK:]


def finish_kernel(both_ref, raw_ref, scale_ref, left_ref, right_ref):
    rows, cols = raw_ref.shape[1], scale_ref.shape[1]
    inverse = inverse_factor(both_ref[:, cols:])
    sides = jnp.concatenate([raw_ref[...], both_ref[:, :cols] * scale_ref[...]], axis=1)
    solved = lax.dot_general(
        inverse, sides, NN, precision=lax.Precision.HIGHEST, preferred_element_type=jnp.float32
    )
    left_ref[...] = solved[:, :rows]
    right_ref[...] = solved[:, rows:]


def groups(*order, first_x=FIRST_X, first_z=FIRST_Z):
    sizes = dict(zip("xzc", GRID))
    fixed = [name for name in "xzc" if name not in order]

    def lists(names):
        return itertools.product(*[range(sizes[name]) for name in names])

    def index(at):
        x, z = (at["x"] + first_x) % sizes["x"], (at["z"] + first_z) % sizes["z"]
        return (x * sizes["z"] + z) * sizes["c"] + 1 - at["c"]

    return [[index(dict(zip(fixed, f)) | dict(zip(order, m))) for m in lists(order)] for f in lists(fixed)]


def exchange(x, axis, members):
    return lax.all_to_all(x, axis, 0, 0, axis_index_groups=members)


def spread(x, axis, members):
    return exchange(jnp.broadcast_to(x[None], (len(members[0]),) + x.shape), axis, members)


def body(behaviour, panel):
    feats = lax.axis_size("feat")
    rows, cols = behaviour.shape
    assert rows == feats * LANES and feats == 8
    every, near, far = groups("x", "z", "c"), groups("x", "c"), groups("z", first_z=5)
    feat = [[(i + FIRST_Y) % feats for i in range(feats)]]
    f32 = jnp.float32
    shape = jax.ShapeDtypeStruct

    sums = call(
        column_kernel, shape((len(every[0]), cols // LANES, LANES), f32), (behaviour,), "columns", rows * cols, 4 * rows * cols
    )
    sums = exchange(sums, "cand", every)
    part, row_sums, col_scale = call(
        project_kernel,
        (shape((feats, RANK, LANES), f32), shape((feats, LANES), f32), shape((1, cols), f32)),
        (behaviour, panel.T, sums),
        "project",
        6 * rows * cols * PAD,
        4 * rows * cols,
    )
    part = exchange(part, "feat", feat)
    share = call(
        share_kernel, shape((feats, PAD, LANES), f32), (part, row_sums), "share", part.size, 8 * part.size
    )
    whole = exchange(share, "feat", feat)
    both, raw = call(
        reduce_kernel,
        (shape((RANK, cols + LANES), f32), shape((RANK, rows), f32)),
        (behaviour, whole),
        "reduce",
        6 * rows * cols * RANK,
        4 * rows * cols,
    )
    both = exchange(both.reshape(len(near[0]), -1, cols + LANES), "cand", near)
    line = jnp.sum(both, axis=0)
    line = jnp.sum(spread(line, "cand", far), axis=0)
    both = spread(line, "cand", near).reshape(RANK, cols + LANES)
    left, right = call(
        finish_kernel,
        (shape((RANK, rows), f32), shape((RANK, cols), f32)),
        (both, raw, col_scale),
        "finish",
        6 * RANK * RANK * (rows + cols),
        8 * RANK * (rows + cols),
    )
    return (left.T, right.T)


def solution(mesh):
    assert GRID[0] * GRID[1] * GRID[2] == mesh.shape["cand"]
    in_specs = (P("cand", "feat"), P("feat", None))
    out_specs = (P("cand", None), P("feat", None))
    return jax.shard_map(body, mesh=mesh, in_specs=in_specs, out_specs=out_specs, check_vma=False)
```
